32 devices in a mesh: group: 4 (over x, core), mp: 8 (over z, y).
Axes of the slice: x: 2, y: 2, z: 4, core: 2. Of those that a mesh axis runs over, the one named last changes fastest.
Arguments:
- tokens: bfloat16 [4096, 8192], P(('group', 'mp')), may hold values from -36 to 36
- cached_update: bfloat16 [4096, 8192], P('group', 'mp'), may hold values from -3 to 3
- norm_gain: float32 [8192], replicated, may hold values from 0.25 to 1.75
- gate_weight: bfloat16 [8192, 14336], P('group', 'mp'), may hold values from -0.0625 to 0.0625
- up_weight: bfloat16 [8192, 14336], P('group', 'mp'), may hold values from -0.0625 to 0.0625
- down_weight: bfloat16 [14336, 8192], P('mp', 'group'), may hold values from -0.0625 to 0.0625
- stale_blocks: int32 [4, 2], P('group'), may hold values from -1 to 7, as said below
- stale_count: int32 [4], replicated, may hold values from 0 to 2, as said below
- lengths: int32 [4], P('group'), may hold values from 512 to 1024, as said below
Outputs:
- refreshed: bfloat16 [4096, 8192], P('group', 'mp')
The draws below stay inside these ranges and needn't reach their ends.
Inputs may be any that keep to these rules, and one draw needn't show every extreme that they name: `stale_count`: the counts sum to exactly 4. At least a quarter of the groups have 2, at least a quarter have none. A group's count never exceeds the number of its blocks that begin below its length. `stale_blocks`: row g holds stale_count[g] distinct block numbers, each of a block that begins below lengths[g], in any order, then -1 in the other places. Some group lists block 7. `lengths`: some request has 1024 tokens.
All inputs are finite; a program needn't handle non-finite values.
Results may differ from the reference program's by a relative error of at most 0.0035.
Values may be sent and summed in bfloat16 or wider, within the bound.
A program may use at most 256 MiB of HBM per device.

```python
import math
import jax
import jax.numpy as jnp
from jax import lax

D = 8192
FF = 14336
BLK = 128
AVGB = 1
MAXB = 2
SEQ = 1024
BLOCKS = 8
ROWS = 4096
STALE_ALL = 4
N_GROUP = 4


def stale_plan(key):
    base_key = jax.random.fold_in(key, 11)
    key_order = jax.random.fold_in(base_key, 0)
    key_shift = jax.random.fold_in(base_key, 1)
    key_length = jax.random.fold_in(base_key, 2)
    key_score = jax.random.fold_in(base_key, 4)
    quarter = N_GROUP // 4
    order_ids = jax.random.permutation(key_order, N_GROUP)
    shifts = jax.random.randint(key_shift, (quarter,), 0, AVGB + 1)
    middle = jnp.stack([AVGB + shifts, AVGB - shifts], axis=1).reshape(-1)
    counts_pos = jnp.concatenate([jnp.full((quarter,), MAXB, jnp.int32), jnp.zeros((quarter,), jnp.int32), middle.astype(jnp.int32)])
    counts = jnp.zeros((N_GROUP,), jnp.int32).at[order_ids].set(counts_pos)
    lengths_drawn = jax.random.randint(key_length, (N_GROUP,), SEQ // 2, SEQ + 1)
    full_at = order_ids[0]
    group_range = jnp.arange(N_GROUP, dtype=jnp.int32)
    lengths_drawn = jnp.where(group_range == full_at, SEQ, lengths_drawn).astype(jnp.int32)
    live_blocks = (lengths_drawn + BLK - 1) // BLK
    scores = jax.random.randint(key_score, (N_GROUP, BLOCKS), 1, 1 << 20)
    block_ids = jnp.arange(BLOCKS, dtype=jnp.int32)
    forced = (group_range[:, None] == full_at) & (block_ids[None, :] == BLOCKS - 1)
    scores = jnp.where(forced, 0, scores)
    keyed = jnp.where(block_ids[None, :] < live_blocks[:, None], scores, 1 << 21) * BLOCKS + block_ids[None, :]
    ranked = jnp.argsort(keyed, axis=1, stable=True)[:, :MAXB].astype(jnp.int32)
    listed = jnp.where(jnp.arange(MAXB)[None, :] < counts[:, None], ranked, -1).astype(jnp.int32)
    return (counts, lengths_drawn, listed)


def draw_stale_blocks(key, part):
    return stale_plan(key)[2]


def draw_stale_count(key, part):
    return stale_plan(key)[0]


def draw_lengths(key, part):
    return stale_plan(key)[1]


def draw_tokens(key, part):
    key_rows, key_cols, key_base = jax.random.split(key, 3)
    row_scale = jnp.exp(jax.random.uniform(key_rows, (ROWS, 1), minval=math.log(0.3), maxval=math.log(3.0)))
    col_scale = jnp.exp(jax.random.uniform(key_cols, (1, D), minval=math.log(0.3), maxval=math.log(3.0)))
    base_vals = jnp.clip(jax.random.normal(key_base, (ROWS, D)), -4.0, 4.0)
    return (base_vals * row_scale * col_scale).astype(jnp.bfloat16)


def raised(array, key, source, target, shards_of, factor):
    owner, partner = [(jnp.arange(array.shape[dim]) // (array.shape[dim] // shards_of)).reshape([-1 if axis == dim else 1 for axis in range(array.ndim)]) for dim in (source, target)]
    chosen = jax.random.permutation(key, shards_of)[partner]
    strong = (owner == chosen) | (owner == (partner + shards_of // 2) % shards_of)
    return jnp.where(strong, factor * array, array)


def shard_levels(own_key, extent, shards, low, top_value):
    factor_of, own = 1.0, jax.random.fold_in(own_key, 6)
    for dim, blocks in shards:
        steps = jnp.exp(jax.random.uniform(jax.random.fold_in(own, dim), (blocks,), jnp.float32, low / len(shards), top_value / len(shards)))
        factor_of = factor_of * jnp.repeat(steps, extent[dim] // blocks).reshape([-1 if axis == dim else 1 for axis in range(len(extent))])
    return factor_of


def bell_draw(stream_key, extent, scale, most, shards=(), held_as=jnp.bfloat16):
    entries = scale * jax.random.normal(stream_key, extent, jnp.float32)
    if shards:
        entries = entries * shard_levels(stream_key, extent, shards, -0.22, 0.18)
    return jnp.clip(entries, -most, most).astype(held_as)


def bell_draw_with(rng, extent, width, reach, cuts, heavy, held_as=jnp.bfloat16):
    result = width * jax.random.normal(rng, extent, jnp.float32)
    if cuts:
        result = result * shard_levels(rng, extent, cuts, -0.22, 0.18)
    return jnp.clip(raised(result, jax.random.fold_in(rng, 3), *heavy), -reach, reach).astype(held_as)


def setup_inputs(seed: int = 0) -> dict:
    key_list = jax.random.split(jax.random.key(seed), 10)
    return {
        "tokens": draw_tokens(jax.random.fold_in(key_list[9], 71), 0),
        "cached_update": bell_draw(key_list[1], (ROWS, D), 0.5, 3.0, ((0, 4), (1, 8))),
        "norm_gain": jnp.clip(1.0 + 0.15 * jax.random.normal(key_list[2], (D,), jnp.float32), 0.25, 1.75),
        "gate_weight": bell_draw(key_list[3], (D, FF), D ** -0.5, 0.0625, ((0, 4), (1, 8))),
        "up_weight": bell_draw(key_list[4], (D, FF), D ** -0.5, 0.0625, ((0, 4), (1, 8))),
        "down_weight": bell_draw_with(key_list[5], (FF, D), FF ** -0.5, 0.0625, ((0, 8), (1, 4)), (0, 1, 8, 2.0)),
        "stale_blocks": draw_stale_blocks(jax.random.fold_in(key_list[9], 71), 0),
        "stale_count": draw_stale_count(jax.random.fold_in(key_list[9], 71), 0),
        "lengths": draw_lengths(jax.random.fold_in(key_list[9], 71), 0),
    }


epsilon = 1e-05

def normalize(row_data, norm_gain):
    values = row_data.astype(jnp.float32)
    mean_sq = lax.optimization_barrier(jnp.mean(values * values, axis=-1, keepdims=True))
    return (values * lax.rsqrt(mean_sq + epsilon) * norm_gain).astype(jnp.bfloat16)

def reference(tokens, cached_update, norm_gain, gate_weight, up_weight, down_weight, stale_blocks, stale_count, lengths):
    count_ends = jnp.cumsum(stale_count).astype(jnp.int32)
    count_starts = count_ends - stale_count
    item_ids = jnp.arange(STALE_ALL, dtype=jnp.int32)
    owner_ids = lax.optimization_barrier(jnp.sum((count_ends[None, :] <= item_ids[:, None]).astype(jnp.int32), axis=1)).astype(jnp.int32)
    slot_pos = (item_ids - count_starts[owner_ids]).astype(jnp.int32)
    block_ids = stale_blocks[owner_ids, slot_pos].astype(jnp.int32)
    grouped = tokens.reshape(N_GROUP, BLOCKS, BLK, D)
    row_data = grouped[owner_ids, block_ids].reshape(STALE_ALL * BLK, D)
    normed = normalize(row_data, norm_gain)
    gate_vals = jnp.dot(normed, gate_weight, preferred_element_type=jnp.float32)
    up_vals = jnp.dot(normed, up_weight, preferred_element_type=jnp.float32)
    hidden = (jax.nn.silu(gate_vals) * up_vals).astype(jnp.bfloat16)
    update = jnp.dot(hidden, down_weight, preferred_element_type=jnp.float32)
    merged = cached_update.reshape(N_GROUP, BLOCKS, BLK, D).astype(jnp.float32)
    merged = merged.at[owner_ids, block_ids].set(update.reshape(STALE_ALL, BLK, D))
    position = jnp.arange(BLOCKS, dtype=jnp.int32)[:, None] * BLK + jnp.arange(BLK, dtype=jnp.int32)[None, :]
    live_rows = position[None, :, :] < lengths[:, None, None]
    refreshed = jnp.where(live_rows[..., None], grouped.astype(jnp.float32) + merged, jnp.float32(0.0))
    return refreshed.astype(jnp.bfloat16).reshape(ROWS, D)
```

```python
import jax
import jax.numpy as jnp
from jax import lax
from jax.sharding import PartitionSpec as P

BLK = 128


epsilon = 1e-05


def body(
    tokens,
    cached_update,
    norm_gain,
    gate_weight,
    up_weight,
    down_weight,
    stale_blocks,
    stale_count,
    lengths,
):
    n_group = lax.axis_size("group")
    n_mp = lax.axis_size("mp")
    split = n_mp // n_group
    group_id = lax.axis_index("group")
    mp_id = lax.axis_index("mp")
    group_ids = jnp.arange(n_group, dtype=jnp.int32)

    values = tokens.astype(jnp.float32)
    mean_sq = jnp.mean(values * values, axis=-1)
    all_mean_sq = lax.all_gather(mean_sq, "mp", axis=0, tiled=True)

    columns = lax.all_to_all(tokens, "mp", split_axis=1, concat_axis=0, tiled=True)
    seq_rows, col_width = columns.shape
    block_total = seq_rows // BLK
    column_blocks = columns.reshape(block_total, BLK, col_width)
    block_ids = jnp.arange(block_total, dtype=jnp.int32)

    count_before = jnp.sum(jnp.where(group_ids < group_id, stale_count, 0))
    own_count = jnp.sum(jnp.where(group_ids == group_id, stale_count, 0))
    own_list = stale_blocks[0]
    positions = jnp.arange(own_list.shape[0], dtype=jnp.int32)
    slot_of = jnp.where(positions < own_count, count_before + positions, -1)
    slots = jnp.arange(n_group, dtype=jnp.int32)
    slot_hits = slot_of[None, :] == slots[:, None]
    slot_block = jnp.sum(jnp.where(slot_hits, own_list[None, :], 0), axis=1)
    slot_own = jnp.any(slot_hits, axis=1)

    scale = lax.rsqrt(all_mean_sq + epsilon).reshape(block_total, BLK)
    own_gain = lax.dynamic_slice_in_dim(norm_gain, mp_id * col_width, col_width)
    placed = []
    for s in range(n_group):
        rows = lax.dynamic_index_in_dim(column_blocks, slot_block[s], 0, keepdims=False)
        row_scale = lax.dynamic_index_in_dim(scale, slot_block[s], 0, keepdims=False)
        normed = rows.astype(jnp.float32) * row_scale[:, None] * own_gain
        placed.append(jnp.where(slot_own[s], normed, 0.0).astype(jnp.bfloat16))
    placed = jnp.stack(placed)
    slot_rows = lax.psum_scatter(placed, "group", scatter_dimension=0, tiled=True)[0]

    pairs = [
        (s * n_mp + m, (m // split) * n_mp + s * split + m % split)
        for s in range(n_group)
        for m in range(n_mp)
    ]
    chunk_rows = lax.ppermute(slot_rows, ("group", "mp"), pairs)
    gathered = lax.all_gather(chunk_rows, "mp", axis=0)
    gathered = gathered.reshape(n_group, split, BLK, col_width)
    normed = gathered.transpose(0, 2, 1, 3).reshape(n_group * BLK, split * col_width)

    gate_part = jnp.dot(normed, gate_weight, preferred_element_type=jnp.float32)
    up_part = jnp.dot(normed, up_weight, preferred_element_type=jnp.float32)
    gate_vals = lax.psum_scatter(
        gate_part.astype(jnp.bfloat16), "group", scatter_dimension=0, tiled=True
    ).astype(jnp.float32)
    up_vals = lax.psum_scatter(
        up_part.astype(jnp.bfloat16), "group", scatter_dimension=0, tiled=True
    ).astype(jnp.float32)
    hidden = (jax.nn.silu(gate_vals) * up_vals).astype(jnp.bfloat16)
    hidden = lax.all_gather(hidden, "group", axis=0, tiled=True)

    partial_value = jnp.dot(hidden, down_weight, preferred_element_type=jnp.float32)
    partial_value = partial_value.astype(jnp.bfloat16)
    pieces = partial_value.reshape(n_group, BLK, split, col_width).transpose(0, 2, 1, 3)
    pieces = pieces.reshape(n_group * split, BLK, col_width)
    piece = lax.psum_scatter(pieces, "mp", scatter_dimension=0, tiled=True)[0]
    piece = lax.ppermute(piece, ("group", "mp"), [(b, a) for a, b in pairs])
    update = lax.all_gather(piece, "group", axis=0)

    listed = (own_list[None, :] == block_ids[:, None]) & (positions < own_count)[None, :]
    stale = jnp.any(listed, axis=1)
    block_slot = jnp.sum(jnp.where(listed, slot_of[None, :], 0), axis=1)
    cache_blocks = cached_update.reshape(block_total, BLK, col_width)
    outs = []
    for b in range(block_total):
        fresh = lax.dynamic_index_in_dim(update, block_slot[b], 0, keepdims=False)
        merged = jnp.where(stale[b], fresh, cache_blocks[b]).astype(jnp.float32)
        live = b * BLK + jnp.arange(BLK, dtype=jnp.int32) < lengths[0]
        total = column_blocks[b].astype(jnp.float32) + merged
        outs.append(jnp.where(live[:, None], total, 0.0).astype(jnp.bfloat16))
    return jnp.concatenate(outs, axis=0)


def solution(mesh):
    in_specs = (
        P(("group", "mp"), None),
        P("group", "mp"),
        P(),
        P("group", "mp"),
        P("group", "mp"),
        P("mp", "group"),
        P("group", None),
        P(),
        P("group"),
    )
    out_specs = P("group", "mp")
    return jax.shard_map(body, mesh=mesh, in_specs=in_specs, out_specs=out_specs, check_vma=False)
```

```python
import functools

import jax
import jax.numpy as jnp
from jax import lax
from jax.experimental import pallas as pl
from jax.experimental.pallas import tpu as pltpu
from jax.sharding import PartitionSpec as P

BLK = 128


epsilon = 1e-05


MESH = pl.DeviceIdType.MESH


def enter(axis, peers):
    barrier = pltpu.get_barrier_semaphore()
    for peer in peers:
        pl.semaphore_signal(barrier, inc=1, device_id={axis: peer}, device_id_type=MESH)
    pl.semaphore_wait(barrier, len(peers))


def swap_kernel(axis, n, count, *refs):
    sources, targets, (send_sem, recv_sem) = refs[:count], refs[count : 2 * count], refs[2 * count :]
    me = lax.axis_index(axis)
    peers = [lax.rem(me + k, n) for k in range(1, n)]
    enter(axis, peers)
    copies = []
    for k, peer in enumerate(peers):
        for i in range(count):
            copy = pltpu.make_async_remote_copy(
                src_ref=sources[i].at[peer],
                dst_ref=targets[i].at[k],
                send_sem=send_sem.at[i, k],
                recv_sem=recv_sem.at[i, k],
                device_id={axis: peer},
                device_id_type=MESH,
            )
            copy.start()
            copies.append(copy)
    for copy in copies:
        copy.wait()


def sum_scatter(arrays, axis, n, call_id):
    count = len(arrays)
    got = pl.pallas_call(
        functools.partial(swap_kernel, axis, n, count),
        out_shape=[jax.ShapeDtypeStruct((n - 1,) + a.shape[1:], a.dtype) for a in arrays],
        in_specs=[pl.BlockSpec(memory_space=pl.ANY)] * count,
        out_specs=[pl.BlockSpec(memory_space=pl.ANY)] * count,
        scratch_shapes=[
            pltpu.SemaphoreType.DMA((count, n - 1)),
            pltpu.SemaphoreType.DMA((count, n - 1)),
        ],
        compiler_params=pltpu.CompilerParams(collective_id=call_id, has_side_effects=True),
    )(*arrays)
    me = lax.axis_index(axis)
    sums = []
    for array, parts in zip(arrays, got):
        total = lax.dynamic_index_in_dim(array, me, 0, keepdims=False).astype(jnp.float32)
        for k in range(n - 1):
            total = total + parts[k].astype(jnp.float32)
        sums.append(total)
    return sums


def spread_kernel(axis, n, x_ref, out_ref, own_sem, far_send, far_recv, near_send, near_recv):
    me = lax.axis_index(axis)
    far, near = lax.div(me, 2), lax.rem(me, 2)
    n_far = n // 2
    partner = far * 2 + (1 - near)
    others = [lax.rem(far + k, n_far) * 2 + near for k in range(1, n_far)]
    enter(axis, others + [partner])

    def send(source, slot, send_sem, recv_sem, peer):
        copy = pltpu.make_async_remote_copy(
            src_ref=source,
            dst_ref=out_ref.at[slot],
            send_sem=send_sem,
            recv_sem=recv_sem,
            device_id={axis: peer},
            device_id_type=MESH,
        )
        copy.start()
        return copy

    far_copies = [
        send(x_ref, me, far_send.at[k], far_recv.at[k], peer) for k, peer in enumerate(others)
    ]
    near_copies = [send(x_ref, me, near_send.at[0], near_recv.at[0], partner)]
    own = pltpu.make_async_copy(x_ref, out_ref.at[me], own_sem)
    own.start()
    for k in range(1, n_far):
        far_copies[k - 1].wait_recv()
        slot = lax.rem(far + (n_far - k), n_far) * 2 + near
        near_copies.append(
            send(out_ref.at[slot], slot, near_send.at[k], near_recv.at[k], partner)
        )
    own.wait()
    for copy in far_copies:
        copy.wait_send()
    for copy in near_copies:
        copy.wait()


def gather(x, axis, n, call_id):
    return pl.pallas_call(
        functools.partial(spread_kernel, axis, n),
        out_shape=jax.ShapeDtypeStruct((n,) + x.shape, x.dtype),
        in_specs=[pl.BlockSpec(memory_space=pltpu.VMEM)],
        out_specs=pl.BlockSpec(memory_space=pl.ANY),
        scratch_shapes=[
            pltpu.SemaphoreType.DMA,
            pltpu.SemaphoreType.DMA((n // 2 - 1,)),
            pltpu.SemaphoreType.DMA((n // 2 - 1,)),
            pltpu.SemaphoreType.DMA((n // 2,)),
            pltpu.SemaphoreType.DMA((n // 2,)),
        ],
        compiler_params=pltpu.CompilerParams(collective_id=call_id, has_side_effects=True),
    )(x)


def merge_kernel(slot_ref, stale_ref, length_ref, rows_ref, cache_ref, update_ref, out_ref):
    b = pl.program_id(0)
    fresh = update_ref[...].astype(jnp.float32)
    cached = cache_ref[...].astype(jnp.float32)
    merged = jnp.where(stale_ref[b] > 0, fresh, cached)
    row = b * BLK + lax.broadcasted_iota(jnp.int32, out_ref.shape, 0)
    total = rows_ref[...].astype(jnp.float32) + merged
    out_ref[...] = jnp.where(row < length_ref[0], total, 0.0).astype(out_ref.dtype)


def merge(columns, cached_update, update, block_slot, stale, lengths):
    width = columns.shape[1]
    block = pl.BlockSpec((BLK, width), lambda b, *_: (b, 0))
    picked = pl.BlockSpec((None, BLK, width), lambda b, slot, *_: (slot[b], 0, 0))
    return pl.pallas_call(
        merge_kernel,
        out_shape=jax.ShapeDtypeStruct(columns.shape, columns.dtype),
        grid_spec=pltpu.PrefetchScalarGridSpec(
            num_scalar_prefetch=3,
            grid=(columns.shape[0] // BLK,),
            in_specs=[block, block, picked],
            out_specs=block,
        ),
    )(block_slot, stale, lengths, columns, cached_update, update)


def body(
    tokens,
    cached_update,
    norm_gain,
    gate_weight,
    up_weight,
    down_weight,
    stale_blocks,
    stale_count,
    lengths,
):
    n_group = lax.axis_size("group")
    n_mp = lax.axis_size("mp")
    split = n_mp // n_group
    group_id = lax.axis_index("group")
    mp_id = lax.axis_index("mp")
    group_ids = jnp.arange(n_group, dtype=jnp.int32)

    values = tokens.astype(jnp.float32)
    mean_sq = jnp.mean(values * values, axis=-1)
    all_mean_sq = lax.all_gather(mean_sq, "mp", axis=0, tiled=True)

    columns = lax.all_to_all(tokens, "mp", split_axis=1, concat_axis=0, tiled=True)
    seq_rows, col_width = columns.shape
    block_total = seq_rows // BLK
    column_blocks = columns.reshape(block_total, BLK, col_width)
    block_ids = jnp.arange(block_total, dtype=jnp.int32)

    count_before = jnp.sum(jnp.where(group_ids < group_id, stale_count, 0))
    own_count = jnp.sum(jnp.where(group_ids == group_id, stale_count, 0))
    own_list = stale_blocks[0]
    positions = jnp.arange(own_list.shape[0], dtype=jnp.int32)
    slot_of = jnp.where(positions < own_count, count_before + positions, -1)
    slots = jnp.arange(n_group, dtype=jnp.int32)
    slot_hits = slot_of[None, :] == slots[:, None]
    slot_block = jnp.sum(jnp.where(slot_hits, own_list[None, :], 0), axis=1)
    slot_own = jnp.any(slot_hits, axis=1)

    scale = lax.rsqrt(all_mean_sq + epsilon).reshape(block_total, BLK)
    own_gain = lax.dynamic_slice_in_dim(norm_gain, mp_id * col_width, col_width)
    placed = []
    for s in range(n_group):
        rows = lax.dynamic_index_in_dim(column_blocks, slot_block[s], 0, keepdims=False)
        row_scale = lax.dynamic_index_in_dim(scale, slot_block[s], 0, keepdims=False)
        normed = rows.astype(jnp.float32) * row_scale[:, None] * own_gain
        placed.append(jnp.where(slot_own[s], normed, 0.0).astype(jnp.bfloat16))
    placed = jnp.stack(placed)
    slot_rows = sum_scatter([placed], "group", n_group, 0)[0].astype(jnp.bfloat16)

    pairs = [
        (s * n_mp + m, (m // split) * n_mp + s * split + m % split)
        for s in range(n_group)
        for m in range(n_mp)
    ]
    chunk_rows = lax.ppermute(slot_rows, ("group", "mp"), pairs)
    gathered = gather(chunk_rows, "mp", n_mp, 1)
    gathered = gathered.reshape(n_group, split, BLK, col_width)
    normed = gathered.transpose(0, 2, 1, 3).reshape(n_group * BLK, split * col_width)

    gate_part = jnp.dot(normed, gate_weight, preferred_element_type=jnp.float32)
    up_part = jnp.dot(normed, up_weight, preferred_element_type=jnp.float32)
    parts = [
        part.astype(jnp.bfloat16).reshape(n_group, BLK, part.shape[1])
        for part in (gate_part, up_part)
    ]
    gate_vals, up_vals = sum_scatter(parts, "group", n_group, 2)
    hidden = (jax.nn.silu(gate_vals) * up_vals).astype(jnp.bfloat16)
    hidden = gather(hidden, "group", n_group, 3).reshape(n_group * BLK, hidden.shape[1])

    partial_value = jnp.dot(hidden, down_weight, preferred_element_type=jnp.float32)
    partial_value = partial_value.astype(jnp.bfloat16)
    pieces = partial_value.reshape(n_group, BLK, split, col_width).transpose(0, 2, 1, 3)
    pieces = pieces.reshape(n_group * split, BLK, col_width)
    piece = sum_scatter([pieces], "mp", n_mp, 4)[0].astype(jnp.bfloat16)
    piece = lax.ppermute(piece, ("group", "mp"), [(b, a) for a, b in pairs])
    update = gather(piece, "group", n_group, 5)

    listed = (own_list[None, :] == block_ids[:, None]) & (positions < own_count)[None, :]
    stale = jnp.any(listed, axis=1)
    block_slot = jnp.sum(jnp.where(listed, slot_of[None, :], 0), axis=1)
    return merge(columns, cached_update, update, block_slot, stale.astype(jnp.int32), lengths)


def solution(mesh):
    in_specs = (
        P(("group", "mp"), None),
        P("group", "mp"),
        P(),
        P("group", "mp"),
        P("group", "mp"),
        P("mp", "group"),
        P("group", None),
        P(),
        P("group"),
    )
    out_specs = P("group", "mp")
    return jax.shard_map(body, mesh=mesh, in_specs=in_specs, out_specs=out_specs, check_vma=False)
```
